32 devices in a mesh: blk: 8 (over y, x, core), member: 4 (over z).
Axes of the slice: x: 2, y: 2, z: 4, core: 2. Of those that a mesh axis runs over, the one named last changes fastest.
Arguments:
- coords: float32 [2048, 64], P(('blk', 'member')), may hold values from -6 to 6
- codes: int32 [2048, 4, 512], P('blk', 'member'), may hold values from 0 to 255
- classes: int32 [2048, 4, 512], P('blk', 'member'), may hold values from 0 to 3
Outputs:
- final_coords: float32 [2048, 64], P(('blk', 'member'))
The draws below stay inside these ranges and needn't reach their ends.
All inputs are finite; a program needn't handle non-finite values.
Results may differ from the reference program's by a relative error of at most 0.0003.
Values sent between devices are 32-bit elements; how exact they have to be, the bound alone decides.
A program may use at most 64 MiB of HBM per device.

```python
import jax
import jax.numpy as jnp
from jax import lax

D = 64
ROWS_DEV = 64
ITERS = 3
NPTS = 2048
N_BLK = 8
N_MEMBER = 4


def set_ends(values, key, low, largest):
    longest = values.shape.index(max(values.shape))
    spots = []
    for shift in (0, 1):
        where = [jax.random.randint(jax.random.fold_in(key, axis), (), 0, length) for axis, length in enumerate(values.shape)]
        where[longest] = (where[longest] + shift) % values.shape[longest]
        spots.append(tuple(where))
    return values.at[spots[0]].set(low).at[spots[1]].set(largest)


def steps_of(own_key, extent, pieces, smallest, top_value):
    def one(axis_at, parts):
        heights = jax.random.uniform(jax.random.fold_in(jax.random.fold_in(own_key, 6), axis_at), (parts,), jnp.float32, smallest / len(pieces), top_value / len(pieces))
        return jnp.repeat(jnp.exp(heights), extent[axis_at] // parts).reshape((-1,) + (1,) * (len(extent) - axis_at - 1))

    loudness = one(*pieces[0])
    for cut in pieces[1:]:
        loudness = loudness * one(*cut)
    return loudness


def normal_values(stream_key, extent, deviation, limit, split=(), kind=jnp.bfloat16):
    loudness = steps_of(stream_key, extent, split, -0.22, 0.18) if split else 1.0
    values = jax.random.normal(stream_key, extent, jnp.float32) * deviation * loudness
    return jnp.minimum(jnp.maximum(values, -limit), limit).astype(kind)


def setup_inputs(seed: int = 0) -> dict:
    keys = jax.random.split(jax.random.key(seed), 4)
    coords = normal_values(keys[0], (NPTS, D), 1.0, 6.0, ((0, 32),), jnp.float32)
    codes = set_ends(jax.random.randint(keys[1], (NPTS, N_MEMBER, N_BLK * ROWS_DEV), 0, 256), jax.random.fold_in(keys[1], 1), 0, 255).astype(jnp.int32)
    classes = set_ends(jax.random.randint(keys[2], (NPTS, N_MEMBER, N_BLK * ROWS_DEV), 0, 4), jax.random.fold_in(keys[2], 1), 0, 3).astype(jnp.int32)
    return {"coords": coords, "codes": codes, "classes": classes}


code_step = 0.1
epsilon = 1e-06

def reference(coords, codes, classes):
    total = coords.shape[0]
    band_len = ROWS_DEV * N_MEMBER
    code_rows = codes.reshape(total, N_MEMBER, N_BLK, ROWS_DEV).transpose(0, 2, 1, 3).reshape(total, total)
    class_rows = classes.reshape(total, N_MEMBER, N_BLK, ROWS_DEV).transpose(0, 2, 1, 3).reshape(total, total)
    col_ids = jnp.arange(total, dtype=jnp.int32)

    def update(points):
        norms = lax.optimization_barrier(jnp.sum(points * points, axis=1))

        def one_band(index):
            start = (index * band_len).astype(jnp.int32)
            band = lax.dynamic_slice_in_dim(points, start, band_len, 0)
            code_tile = lax.dynamic_slice_in_dim(code_rows, start, band_len, 0)
            class_tile = lax.dynamic_slice_in_dim(class_rows, start, band_len, 0)
            row_ids = start + jnp.arange(band_len, dtype=jnp.int32)
            self_pair = row_ids[:, None] == col_ids[None, :]
            weights = jnp.where(self_pair, jnp.float32(0.0), 1.0 / (1.0 + class_tile.astype(jnp.float32)))
            targeted = weights * (code_tile.astype(jnp.float32) + 1.0) * code_step
            gram = jnp.dot(band, points.T, precision=lax.Precision.HIGHEST)
            dist_sq = lax.optimization_barrier(jnp.sum(band * band, axis=1))[:, None] + norms[None, :] - 2.0 * gram
            dist_sq = jnp.where(self_pair, jnp.float32(1.0), dist_sq)
            ratio = targeted / jnp.sqrt(dist_sq + epsilon)
            numer = jnp.dot(weights - ratio, points, precision=lax.Precision.HIGHEST)
            return (numer + band * lax.optimization_barrier(jnp.sum(ratio, axis=1))[:, None]) / lax.optimization_barrier(jnp.sum(weights, axis=1))[:, None]
        result = lax.map(one_band, jnp.arange(N_BLK, dtype=jnp.int32))
        return result.reshape(total, points.shape[1])
    for step in range(ITERS):
        coords = update(coords)
    return coords
```

```python
import functools

import jax
import jax.numpy as jnp
from jax import lax
from jax.experimental import pallas as pl
from jax.experimental.pallas import tpu as pltpu
from jax.sharding import PartitionSpec as P

ITERS = 3
code_step = 0.1
epsilon = 1e-06

F32 = jnp.float32
BF16 = jnp.bfloat16
LANES = 128


def split3(x):
    high = x.astype(BF16).astype(F32)
    rest = x - high
    mid = rest.astype(BF16).astype(F32)
    return high, mid, rest - mid


def doubled(packed):
    n, half, width = packed.shape
    low = lax.broadcasted_iota(jnp.int32, packed.shape, 2) < width // 2
    swapped = jnp.concatenate([packed[..., width // 2:], packed[..., : width // 2]], axis=2)
    return jnp.concatenate([jnp.where(low, packed, swapped), jnp.where(low, swapped, packed)], axis=1).reshape(n * 2 * half, width)


def pack(twice):
    half, width = twice.shape[0] // 2, twice.shape[1]
    low = lax.broadcasted_iota(jnp.int32, (half, width), 1) < width // 2
    return jnp.where(low, twice[:half], twice[half:])


def factors(twice):
    low = lax.broadcasted_iota(jnp.int32, twice.shape, 1) < twice.shape[1] // 2
    norm = 0.5 * jnp.sum(twice * twice, axis=1, keepdims=True)
    return low, split3(twice), split3(norm)


def norm_lanes(norm, rows, first, second):
    lane = lax.broadcasted_iota(jnp.int32, (rows, LANES), 1)
    ones = jnp.where((lane >= second) & (lane < second + 3), 1.0, 0.0)
    n0, n1, n2 = norm
    return jnp.where(lane == first, n0, jnp.where(lane == first + 1, n1, jnp.where(lane == first + 2, n2, ones))).astype(BF16)


def row_side(twice):
    low, (h, m, l), norm = factors(twice)
    parts = [(-2.0 * h).astype(BF16), (-2.0 * m).astype(BF16), (-2.0 * jnp.where(low, h, l)).astype(BF16)]
    return jnp.concatenate(parts + [norm_lanes(norm, twice.shape[0], 3, 0)], axis=1)


def column_side(twice):
    low, (h, m, l), norm = factors(twice)
    hm = jnp.where(low, h, m).astype(BF16)
    gram = jnp.concatenate([hm, hm, jnp.where(low, l, h).astype(BF16), norm_lanes(norm, twice.shape[0], 0, 3)], axis=1)
    return gram, jnp.concatenate([hm, jnp.where(low, l, 0.0).astype(BF16)], axis=1)


def kernel(n_blk, n_mem, coords, codes, classes, out,
           own, columns, band, weights, targets, code_tile, class_tile, part, part_in, wsum, wsum_in,
           load_sem, col_send, col_recv, band_send, band_recv, part_send, part_recv, w_send, w_recv):
    blk, mem = lax.axis_index("blk"), lax.axis_index("member")
    rows, width = coords.shape
    half = rows // 2
    slab = codes.shape[1]
    blks = [lax.rem(blk + k, n_blk) for k in range(1, n_blk)]
    mems = [lax.rem(mem + k, n_mem) for k in range(1, n_mem)]

    loads = [pltpu.make_async_copy(coords, out, load_sem.at[0]),
             pltpu.make_async_copy(codes, code_tile, load_sem.at[1]),
             pltpu.make_async_copy(classes, class_tile, load_sem.at[2])]
    for load in loads:
        load.start()
    barrier = pltpu.get_barrier_semaphore()
    for b in blks:
        pl.semaphore_signal(barrier, inc=1, device_id={"blk": b, "member": mem}, device_id_type=pl.DeviceIdType.MESH)
    for m in mems:
        pl.semaphore_signal(barrier, inc=1, device_id={"blk": blk, "member": m}, device_id_type=pl.DeviceIdType.MESH)

    def send(src, dst, ssem, rsem, b, m):
        return pltpu.make_async_remote_copy(src_ref=src, dst_ref=dst, send_sem=ssem, recv_sem=rsem,
                                            device_id={"blk": b, "member": m}, device_id_type=pl.DeviceIdType.MESH)

    def col_copy(it, b, slot):
        return send(own.at[it], columns.at[it, slot], col_send.at[it, b], col_recv.at[it, slot], b, mem)

    def band_copy(it, m, slot):
        return send(own.at[it], band.at[it, slot], band_send.at[it, m], band_recv.at[it, slot], blk, m)

    def part_copy(it, m, slot):
        return send(part.at[it, m], part_in.at[it, slot], part_send.at[it, m], part_recv.at[it, slot], blk, m)

    def w_copy(m, slot):
        return send(wsum.at[m], wsum_in.at[slot], w_send.at[m], w_recv.at[slot], blk, m)

    def spread(it, packed):
        own[it] = packed
        for b in blks:
            col_copy(it, b, blk).start()
        for m in mems:
            band_copy(it, m, mem).start()
        columns[it, blk] = packed
        band[it, mem] = packed

    loads[0].wait()
    start = out[...]
    first = jnp.concatenate([start[:half], start[half:]], axis=1)
    pl.semaphore_wait(barrier, n_blk + n_mem - 2)
    spread(0, first)

    loads[1].wait()
    loads[2].wait()
    order = mems + [mem]
    for m in order:
        at = pl.ds(pl.multiple_of(m * rows, rows), rows)
        row = lax.broadcasted_iota(jnp.int32, (rows, slab), 0)
        col = lax.broadcasted_iota(jnp.int32, (rows, slab), 1)
        self_at = jnp.where(m == mem, blk * rows, -slab - rows)
        weight = jnp.where(col == row + self_at, 0.0, 1.0 / (1.0 + class_tile[at, :].astype(F32)))
        weights[at, :] = weight
        targets[at, :] = weight * (code_tile[at, :].astype(F32) + 1.0) * code_step
        total = jnp.broadcast_to(jnp.sum(weight, axis=1, keepdims=True), (rows, 2 * width))
        wsum[m] = pack(total)
    for m in mems:
        w_copy(m, mem).start()

    for it in range(ITERS):
        for b in blks:
            col_copy(it, b, b).wait_recv()
        gram_side, sum_side = column_side(doubled(columns[it]))
        for m in mems:
            band_copy(it, m, m).wait_recv()
        total = None
        for m in order:
            at = pl.ds(pl.multiple_of(m * rows, rows), rows)
            twice = doubled(band[it, pl.ds(m, 1)])
            dist_sq = lax.dot_general(row_side(twice), gram_side, (((1,), (1,)), ((), ())), preferred_element_type=F32)
            ratio = targets[at, :] * lax.rsqrt(jnp.maximum(dist_sq, 0.0) + epsilon)
            pull = weights[at, :] - ratio
            high = pull.astype(BF16)
            low = (pull - high.astype(F32)).astype(BF16)
            sums = jnp.dot(jnp.concatenate([high, low], axis=0), sum_side, preferred_element_type=F32)
            sums = sums[:rows] + sums[rows:]
            sums = sums[:, : 2 * width] + sums[:, 2 * width:]
            sums = sums + jnp.concatenate([sums[:, width:], sums[:, :width]], axis=1)
            total = pack(sums + twice * jnp.sum(ratio, axis=1, keepdims=True))
            if m is not mem:
                part[it, m] = total
                part_copy(it, m, mem).start()
        if it == 0:
            weight_own = wsum[mem]
            for m in mems:
                w_copy(m, m).wait_recv()
                weight_own = weight_own + wsum_in[m]
        for m in mems:
            part_copy(it, m, m).wait_recv()
            total = total + part_in[it, m]
        total = total / weight_own
        if it < ITERS - 1:
            spread(it + 1, total)
    out[...] = jnp.concatenate([total[:, :width], total[:, width:]], axis=0)

    for m in mems:
        w_copy(m, m).wait_send()
    for it in range(ITERS):
        for b in blks:
            col_copy(it, b, b).wait_send()
        for m in mems:
            band_copy(it, m, m).wait_send()
            part_copy(it, m, m).wait_send()


def body(n_blk, n_mem, coords, codes, classes):
    rows, width = coords.shape
    band_len, slab = rows * n_mem, rows * n_blk
    packed = (rows // 2, 2 * width)
    dma = pltpu.SemaphoreType.DMA
    return pl.pallas_call(
        functools.partial(kernel, n_blk, n_mem),
        out_shape=jax.ShapeDtypeStruct((rows, width), F32),
        in_specs=[pl.BlockSpec(memory_space=pl.ANY)] * 3,
        out_specs=pl.BlockSpec(memory_space=pltpu.VMEM),
        scratch_shapes=[
            pltpu.VMEM((ITERS,) + packed, F32),
            pltpu.VMEM((ITERS, n_blk) + packed, F32),
            pltpu.VMEM((ITERS, n_mem) + packed, F32),
            pltpu.VMEM((band_len, slab), F32),
            pltpu.VMEM((band_len, slab), F32),
            pltpu.VMEM((band_len, slab), jnp.int32),
            pltpu.VMEM((band_len, slab), jnp.int32),
            pltpu.VMEM((ITERS, n_mem) + packed, F32),
            pltpu.VMEM((ITERS, n_mem) + packed, F32),
            pltpu.VMEM((n_mem,) + packed, F32),
            pltpu.VMEM((n_mem,) + packed, F32),
            dma((3,)),
            dma((ITERS, n_blk)), dma((ITERS, n_blk)),
            dma((ITERS, n_mem)), dma((ITERS, n_mem)),
            dma((ITERS, n_mem)), dma((ITERS, n_mem)),
            dma((n_mem,)), dma((n_mem,)),
        ],
        compiler_params=pltpu.CompilerParams(collective_id=0, has_side_effects=True),
        name="majorize",
    )(coords, codes.reshape(band_len, slab), classes.reshape(band_len, slab))


def solution(mesh):
    n_blk, n_mem = mesh.shape["blk"], mesh.shape["member"]
    in_specs = (P(("blk", "member"), None), P("blk", "member", None), P("blk", "member", None))
    out_specs = P(("blk", "member"), None)
    return jax.shard_map(functools.partial(body, n_blk, n_mem), mesh=mesh, in_specs=in_specs, out_specs=out_specs, check_vma=False)
```

```python
import functools

import jax
import jax.numpy as jnp
from jax import lax
from jax.experimental import pallas as pl
from jax.experimental.pallas import tpu as pltpu
from jax.sharding import PartitionSpec as P

ITERS = 3
code_step = 0.1
epsilon = 1e-06

F32 = jnp.float32
BF16 = jnp.bfloat16
LANES = 128


def split3(x):
    high = x.astype(BF16).astype(F32)
    rest = x - high
    mid = rest.astype(BF16).astype(F32)
    return high, mid, rest - mid


def doubled(packed):
    n, half, width = packed.shape
    low = lax.broadcasted_iota(jnp.int32, packed.shape, 2) < width // 2
    swapped = jnp.concatenate([packed[..., width // 2:], packed[..., : width // 2]], axis=2)
    return jnp.concatenate([jnp.where(low, packed, swapped), jnp.where(low, swapped, packed)], axis=1).reshape(n * 2 * half, width)


def pack(twice):
    half, width = twice.shape[0] // 2, twice.shape[1]
    low = lax.broadcasted_iota(jnp.int32, (half, width), 1) < width // 2
    return jnp.where(low, twice[:half], twice[half:])


def factors(twice):
    low = lax.broadcasted_iota(jnp.int32, twice.shape, 1) < twice.shape[1] // 2
    norm = 0.5 * jnp.sum(twice * twice, axis=1, keepdims=True)
    return low, split3(twice), split3(norm)


def norm_lanes(norm, rows, first, second):
    lane = lax.broadcasted_iota(jnp.int32, (rows, LANES), 1)
    ones = jnp.where((lane >= second) & (lane < second + 3), 1.0, 0.0)
    n0, n1, n2 = norm
    return jnp.where(lane == first, n0, jnp.where(lane == first + 1, n1, jnp.where(lane == first + 2, n2, ones))).astype(BF16)


def row_side(twice):
    low, (h, m, l), norm = factors(twice)
    parts = [(-2.0 * h).astype(BF16), (-2.0 * m).astype(BF16), (-2.0 * jnp.where(low, h, l)).astype(BF16)]
    return jnp.concatenate(parts + [norm_lanes(norm, twice.shape[0], 3, 0)], axis=1)


def column_side(twice):
    low, (h, m, l), norm = factors(twice)
    hm = jnp.where(low, h, m).astype(BF16)
    gram = jnp.concatenate([hm, hm, jnp.where(low, l, h).astype(BF16), norm_lanes(norm, twice.shape[0], 0, 3)], axis=1)
    return gram, jnp.concatenate([hm, jnp.where(low, l, 0.0).astype(BF16)], axis=1)


def near_first(at, n):
    if n & (n - 1):
        return [lax.rem(at + k, n) for k in range(1, n)]
    flips = [(bit, bit * (1 - 2 * lax.rem(at // bit, 2))) for bit in (1 << i for i in range(n.bit_length() - 1))]
    return [at + sum(flip for bit, flip in flips if k & bit) for k in range(1, n)]


def far_first(at, n):
    low, high, found = 0, n - 1, []
    for _ in range(n - 1):
        pick = (2 * at - low - high + n) // n
        found.append(high + pick * (low - high))
        low, high = low + pick, high - 1 + pick
    return found


def kernel(n_blk, n_mem, coords, codes, classes, out,
           own, columns, band, weights, targets, code_tile, class_tile, gram_side, sum_side, part, part_in, wsum, wsum_in,
           load_sem, col_send, col_recv, band_send, band_recv, part_send, part_recv, w_send, w_recv):
    blk, mem = lax.axis_index("blk"), lax.axis_index("member")
    rows, width = coords.shape
    half = rows // 2
    slab = codes.shape[2]
    blks = near_first(blk, n_blk)
    mems = far_first(mem, n_mem)

    loads = [pltpu.make_async_copy(coords, out, load_sem.at[0]),
             pltpu.make_async_copy(classes.at[:, 0, :], class_tile, load_sem.at[1]),
             pltpu.make_async_copy(codes.at[:, 0, :], code_tile, load_sem.at[2])]
    for load in loads:
        load.start()
    barrier = pltpu.get_barrier_semaphore()
    for b in blks:
        pl.semaphore_signal(barrier, inc=1, device_id={"blk": b, "member": mem}, device_id_type=pl.DeviceIdType.MESH)
    for m in mems:
        pl.semaphore_signal(barrier, inc=1, device_id={"blk": blk, "member": m}, device_id_type=pl.DeviceIdType.MESH)

    def send(src, dst, ssem, rsem, b, m):
        return pltpu.make_async_remote_copy(src_ref=src, dst_ref=dst, send_sem=ssem, recv_sem=rsem,
                                            device_id={"blk": b, "member": m}, device_id_type=pl.DeviceIdType.MESH)

    def col_copy(it, b, slot):
        return send(own.at[it], columns.at[it, slot], col_send.at[it, b], col_recv.at[it, slot], b, mem)

    def band_copy(it, m, slot):
        return send(own.at[it], band.at[it, slot], band_send.at[it, m], band_recv.at[it, slot], blk, m)

    def part_copy(it, m, slot):
        return send(part.at[it, m], part_in.at[it, slot], part_send.at[it, m], part_recv.at[it, slot], blk, m)

    def w_copy(m, slot):
        return send(wsum.at[m], wsum_in.at[slot], w_send.at[m], w_recv.at[slot], blk, m)

    def spread(it, packed):
        own[it] = packed
        for m in mems:
            band_copy(it, m, mem).start()
        for b in reversed(blks):
            col_copy(it, b, blk).start()
        columns[it, blk] = packed
        band[it, mem] = packed

    loads[0].wait()
    start = out[...]
    first = jnp.concatenate([start[:half], start[half:]], axis=1)
    pl.semaphore_wait(barrier, n_blk + n_mem - 2)
    spread(0, first)

    loads[1].wait()
    loads[2].wait()
    order = mems + [mem]
    for m in order:
        at = pl.ds(pl.multiple_of(m * rows, rows), rows)
        row = lax.broadcasted_iota(jnp.int32, (rows, slab), 0)
        col = lax.broadcasted_iota(jnp.int32, (rows, slab), 1)
        self_at = jnp.where(m == mem, blk * rows, -slab - rows)
        weight = jnp.where(col == row + self_at, 0.0, 1.0 / (1.0 + class_tile[at, :].astype(F32)))
        weights[at, :] = weight
        targets[at, :] = weight * (code_tile[at, :].astype(F32) + 1.0) * code_step
        total = jnp.broadcast_to(jnp.sum(weight, axis=1, keepdims=True), (rows, 2 * width))
        wsum[m] = pack(total)
    for m in mems:
        w_copy(m, mem).start()

    for it in range(ITERS):
        for b in [blk] + blks:
            if b is not blk:
                col_copy(it, b, b).wait_recv()
            block = pl.ds(pl.multiple_of(b * rows, rows), rows)
            gram_side[block, :], sum_side[block, :] = column_side(doubled(columns[it, pl.ds(b, 1)]))
        for m in order:
            if m is not mem:
                band_copy(it, m, m).wait_recv()
            at = pl.ds(pl.multiple_of(m * rows, rows), rows)
            twice = doubled(band[it, pl.ds(m, 1)])
            dist_sq = lax.dot_general(row_side(twice), gram_side[...], (((1,), (1,)), ((), ())), preferred_element_type=F32)
            ratio = targets[at, :] * lax.rsqrt(jnp.maximum(dist_sq, 0.0) + epsilon)
            pull = weights[at, :] - ratio
            high = pull.astype(BF16)
            low = (pull - high.astype(F32)).astype(BF16)
            sums = jnp.dot(jnp.concatenate([high, low], axis=0), sum_side[...], preferred_element_type=F32)
            sums = sums[:rows] + sums[rows:]
            sums = sums[:, : 2 * width] + sums[:, 2 * width:]
            sums = sums + jnp.concatenate([sums[:, width:], sums[:, :width]], axis=1)
            packed = pack(sums + twice * jnp.sum(ratio, axis=1, keepdims=True))
            if m is mem:
                total = packed
            else:
                part[it, m] = packed
                part_copy(it, m, mem).start()
        if it == 0:
            weight_own = wsum[mem]
            for m in mems:
                w_copy(m, m).wait_recv()
                weight_own = weight_own + wsum_in[m]
        for m in mems:
            part_copy(it, m, m).wait_recv()
            total = total + part_in[it, m]
        total = total / weight_own
        if it < ITERS - 1:
            spread(it + 1, total)
    out[...] = jnp.concatenate([total[:, :width], total[:, width:]], axis=0)

    for m in mems:
        w_copy(m, m).wait_send()
    for it in range(ITERS):
        for b in blks:
            col_copy(it, b, b).wait_send()
        for m in mems:
            band_copy(it, m, m).wait_send()
            part_copy(it, m, m).wait_send()


def body(n_blk, n_mem, coords, codes, classes):
    rows, width = coords.shape
    band_len, slab = rows * n_mem, rows * n_blk
    packed = (rows // 2, 2 * width)
    dma = pltpu.SemaphoreType.DMA
    return pl.pallas_call(
        functools.partial(kernel, n_blk, n_mem),
        out_shape=jax.ShapeDtypeStruct((rows, width), F32),
        in_specs=[pl.BlockSpec(memory_space=pl.ANY)] * 3,
        out_specs=pl.BlockSpec(memory_space=pltpu.VMEM),
        scratch_shapes=[
            pltpu.VMEM((ITERS,) + packed, F32),
            pltpu.VMEM((ITERS, n_blk) + packed, F32),
            pltpu.VMEM((ITERS, n_mem) + packed, F32),
            pltpu.VMEM((band_len, slab), F32),
            pltpu.VMEM((band_len, slab), F32),
            pltpu.VMEM((band_len, slab), jnp.int32),
            pltpu.VMEM((band_len, slab), jnp.int32),
            pltpu.VMEM((slab, 4 * LANES), BF16),
            pltpu.VMEM((slab, 4 * width), BF16),
            pltpu.VMEM((ITERS, n_mem) + packed, F32),
            pltpu.VMEM((ITERS, n_mem) + packed, F32),
            pltpu.VMEM((n_mem,) + packed, F32),
            pltpu.VMEM((n_mem,) + packed, F32),
            dma((3,)),
            dma((ITERS, n_blk)), dma((ITERS, n_blk)),
            dma((ITERS, n_mem)), dma((ITERS, n_mem)),
            dma((ITERS, n_mem)), dma((ITERS, n_mem)),
            dma((n_mem,)), dma((n_mem,)),
        ],
        compiler_params=pltpu.CompilerParams(collective_id=0, has_side_effects=True),
        name="majorize",
    )(coords, codes, classes)


def solution(mesh):
    n_blk, n_mem = mesh.shape["blk"], mesh.shape["member"]
    in_specs = (P(("blk", "member"), None), P("blk", "member", None), P("blk", "member", None))
    out_specs = P(("blk", "member"), None)
    return jax.shard_map(functools.partial(body, n_blk, n_mem), mesh=mesh, in_specs=in_specs, out_specs=out_specs, check_vma=False)
```

```python
import functools

import jax
import jax.numpy as jnp
from jax import lax
from jax.experimental import pallas as pl
from jax.experimental.pallas import tpu as pltpu
from jax.sharding import PartitionSpec as P

ITERS = 3
code_step = 0.1
epsilon = 1e-06

F32 = jnp.float32
BF16 = jnp.bfloat16
LANES = 128


def split3(x):
    high = x.astype(BF16).astype(F32)
    rest = x - high
    mid = rest.astype(BF16).astype(F32)
    return high, mid, rest - mid


def doubled(packed):
    n, half, width = packed.shape
    low = lax.broadcasted_iota(jnp.int32, packed.shape, 2) < width // 2
    swapped = jnp.concatenate([packed[..., width // 2:], packed[..., : width // 2]], axis=2)
    return jnp.concatenate([jnp.where(low, packed, swapped), jnp.where(low, swapped, packed)], axis=1).reshape(n * 2 * half, width)


def pack(twice):
    half, width = twice.shape[0] // 2, twice.shape[1]
    low = lax.broadcasted_iota(jnp.int32, (half, width), 1) < width // 2
    return jnp.where(low, twice[:half], twice[half:])


def factors(twice):
    low = lax.broadcasted_iota(jnp.int32, twice.shape, 1) < twice.shape[1] // 2
    norm = 0.5 * jnp.sum(twice * twice, axis=1, keepdims=True)
    return low, split3(twice), split3(norm)


def norm_lanes(norm, rows, first, second):
    lane = lax.broadcasted_iota(jnp.int32, (rows, LANES), 1)
    ones = jnp.where((lane >= second) & (lane < second + 3), 1.0, 0.0)
    n0, n1, n2 = norm
    return jnp.where(lane == first, n0, jnp.where(lane == first + 1, n1, jnp.where(lane == first + 2, n2, ones))).astype(BF16)


def row_side(twice):
    low, (h, m, l), norm = factors(twice)
    parts = [(-2.0 * h).astype(BF16), (-2.0 * m).astype(BF16), (-2.0 * jnp.where(low, h, l)).astype(BF16)]
    return jnp.concatenate(parts + [norm_lanes(norm, twice.shape[0], 3, 0)], axis=1)


def column_side(twice):
    low, (h, m, l), norm = factors(twice)
    hm = jnp.where(low, h, m).astype(BF16)
    gram = jnp.concatenate([hm, hm, jnp.where(low, l, h).astype(BF16), norm_lanes(norm, twice.shape[0], 0, 3)], axis=1)
    return gram, jnp.concatenate([hm, jnp.where(low, l, 0.0).astype(BF16)], axis=1)


def near_first(at, n):
    if n & (n - 1):
        return [lax.rem(at + k, n) for k in range(1, n)]
    flips = [(bit, bit * (1 - 2 * lax.rem(at // bit, 2))) for bit in (1 << i for i in range(n.bit_length() - 1))]
    return [at + sum(flip for bit, flip in flips if k & bit) for k in range(1, n)]


def far_first(at, n):
    low, high, found = 0, n - 1, []
    for _ in range(n - 1):
        pick = (2 * at - low - high + n) // n
        found.append(high + pick * (low - high))
        low, high = low + pick, high - 1 + pick
    return found


def kernel(n_blk, n_mem, coords, codes, classes, out,
           own, columns, band, weights, targets, code_tile, class_tile, gram_side, sum_side, part, part_in, wsum, wsum_in,
           load_sem, col_send, col_recv, band_send, band_recv, part_send, part_recv, w_send, w_recv):
    blk, mem = lax.axis_index("blk"), lax.axis_index("member")
    rows, width = coords.shape
    half = rows // 2
    slab = codes.shape[2]
    blks = near_first(blk, n_blk)
    mems = far_first(mem, n_mem)

    loads = [pltpu.make_async_copy(coords, out, load_sem.at[0]),
             pltpu.make_async_copy(classes.at[:, 0, :], class_tile, load_sem.at[1]),
             pltpu.make_async_copy(codes.at[:, 0, :], code_tile, load_sem.at[2])]
    for load in loads:
        load.start()
    barrier = pltpu.get_barrier_semaphore()
    for b in blks:
        pl.semaphore_signal(barrier, inc=1, device_id={"blk": b, "member": mem}, device_id_type=pl.DeviceIdType.MESH)
    for m in mems:
        pl.semaphore_signal(barrier, inc=1, device_id={"blk": blk, "member": m}, device_id_type=pl.DeviceIdType.MESH)

    def send(src, dst, ssem, rsem, b, m):
        return pltpu.make_async_remote_copy(src_ref=src, dst_ref=dst, send_sem=ssem, recv_sem=rsem,
                                            device_id={"blk": b, "member": m}, device_id_type=pl.DeviceIdType.MESH)

    def col_copy(it, b, slot):
        return send(own.at[it], columns.at[it, slot], col_send.at[it, b], col_recv.at[it, slot], b, mem)

    def band_copy(it, m, slot):
        return send(own.at[it], band.at[it, slot], band_send.at[it, m], band_recv.at[it, slot], blk, m)

    def part_copy(it, m, slot):
        return send(part.at[it, m], part_in.at[it, slot], part_send.at[it, m], part_recv.at[it, slot], blk, m)

    def w_copy(m, slot):
        return send(wsum.at[m], wsum_in.at[slot], w_send.at[m], w_recv.at[slot], blk, m)

    def spread(it, packed):
        own[it] = packed
        for m in mems:
            band_copy(it, m, mem).start()
        for b in reversed(blks):
            col_copy(it, b, blk).start()
        columns[it, blk] = packed
        band[it, mem] = packed

    loads[0].wait()
    start = out[...]
    first = jnp.concatenate([start[:half], start[half:]], axis=1)
    pl.semaphore_wait(barrier, n_blk + n_mem - 2)
    spread(0, first)

    loads[1].wait()
    loads[2].wait()
    order = mems + [mem]
    for m in order:
        at = pl.ds(pl.multiple_of(m * rows, rows), rows)
        row = lax.broadcasted_iota(jnp.int32, (rows, slab), 0)
        col = lax.broadcasted_iota(jnp.int32, (rows, slab), 1)
        self_at = jnp.where(m == mem, blk * rows, -slab - rows)
        weight = jnp.where(col == row + self_at, 0.0, 1.0 / (1.0 + class_tile[at, :].astype(F32)))
        weights[at, :] = weight
        targets[at, :] = weight * (code_tile[at, :].astype(F32) + 1.0) * code_step
        total = jnp.broadcast_to(jnp.sum(weight, axis=1, keepdims=True), (rows, 2 * width))
        wsum[m] = pack(total)
    for m in mems:
        w_copy(m, mem).start()

    for it in range(ITERS):
        arriving = [blk] + blks
        for pair in [arriving[k:k + 2] for k in range(0, n_blk, 2)]:
            for b in pair:
                if b is not blk:
                    col_copy(it, b, b).wait_recv()
            gram, sums = column_side(doubled(jnp.concatenate([columns[it, pl.ds(b, 1)] for b in pair], axis=0)))
            for k, b in enumerate(pair):
                block = pl.ds(pl.multiple_of(b * rows, rows), rows)
                gram_side[block, :], sum_side[block, :] = gram[k * rows:(k + 1) * rows], sums[k * rows:(k + 1) * rows]
        for m in mems:
            band_copy(it, m, m).wait_recv()
        for group in [mems, [mem]]:
            ats = [pl.ds(pl.multiple_of(m * rows, rows), rows) for m in group]
            twice = jnp.concatenate([doubled(band[it, pl.ds(m, 1)]) for m in group], axis=0)
            dist_sq = lax.dot_general(row_side(twice), gram_side[...], (((1,), (1,)), ((), ())), preferred_element_type=F32)
            target = jnp.concatenate([targets[at, :] for at in ats], axis=0)
            weight = jnp.concatenate([weights[at, :] for at in ats], axis=0)
            ratio = target * lax.rsqrt(jnp.maximum(dist_sq, 0.0) + epsilon)
            pull = weight - ratio
            high = pull.astype(BF16)
            low = (pull - high.astype(F32)).astype(BF16)
            sums = jnp.dot(jnp.concatenate([high, low], axis=0), sum_side[...], preferred_element_type=F32)
            sums = sums[:rows * len(group)] + sums[rows * len(group):]
            sums = sums[:, : 2 * width] + sums[:, 2 * width:]
            sums = sums + jnp.concatenate([sums[:, width:], sums[:, :width]], axis=1)
            sums = sums + twice * jnp.sum(ratio, axis=1, keepdims=True)
            for at, m in enumerate(group):
                packed = pack(sums[at * rows:(at + 1) * rows])
                if m is mem:
                    total = packed
                else:
                    part[it, m] = packed
                    part_copy(it, m, mem).start()
        if it == 0:
            weight_own = wsum[mem]
            for m in mems:
                w_copy(m, m).wait_recv()
                weight_own = weight_own + wsum_in[m]
        for m in mems:
            part_copy(it, m, m).wait_recv()
            total = total + part_in[it, m]
        total = total / weight_own
        if it < ITERS - 1:
            spread(it + 1, total)
    out[...] = jnp.concatenate([total[:, :width], total[:, width:]], axis=0)

    for m in mems:
        w_copy(m, m).wait_send()
    for it in range(ITERS):
        for b in blks:
            col_copy(it, b, b).wait_send()
        for m in mems:
            band_copy(it, m, m).wait_send()
            part_copy(it, m, m).wait_send()


def body(n_blk, n_mem, coords, codes, classes):
    rows, width = coords.shape
    band_len, slab = rows * n_mem, rows * n_blk
    packed = (rows // 2, 2 * width)
    dma = pltpu.SemaphoreType.DMA
    return pl.pallas_call(
        functools.partial(kernel, n_blk, n_mem),
        out_shape=pltpu.VMEM((rows, width), F32),
        in_specs=[pl.BlockSpec(memory_space=pl.ANY)] * 3,
        out_specs=pl.BlockSpec(memory_space=pltpu.VMEM),
        scratch_shapes=[
            pltpu.VMEM((ITERS,) + packed, F32),
            pltpu.VMEM((ITERS, n_blk) + packed, F32),
            pltpu.VMEM((ITERS, n_mem) + packed, F32),
            pltpu.VMEM((band_len, slab), F32),
            pltpu.VMEM((band_len, slab), F32),
            pltpu.VMEM((band_len, slab), jnp.int32),
            pltpu.VMEM((band_len, slab), jnp.int32),
            pltpu.VMEM((slab, 4 * LANES), BF16),
            pltpu.VMEM((slab, 4 * width), BF16),
            pltpu.VMEM((ITERS, n_mem) + packed, F32),
            pltpu.VMEM((ITERS, n_mem) + packed, F32),
            pltpu.VMEM((n_mem,) + packed, F32),
            pltpu.VMEM((n_mem,) + packed, F32),
            dma((3,)),
            dma((ITERS, n_blk)), dma((ITERS, n_blk)),
            dma((ITERS, n_mem)), dma((ITERS, n_mem)),
            dma((ITERS, n_mem)), dma((ITERS, n_mem)),
            dma((n_mem,)), dma((n_mem,)),
        ],
        compiler_params=pltpu.CompilerParams(collective_id=0, has_side_effects=True),
        name="majorize",
    )(coords, codes, classes)


def solution(mesh):
    n_blk, n_mem = mesh.shape["blk"], mesh.shape["member"]
    in_specs = (P(("blk", "member"), None), P("blk", "member", None), P("blk", "member", None))
    out_specs = P(("blk", "member"), None)
    return jax.shard_map(functools.partial(body, n_blk, n_mem), mesh=mesh, in_specs=in_specs, out_specs=out_specs, check_vma=False)
```

```python
import functools

import jax
import jax.numpy as jnp
from jax import lax
from jax.experimental import pallas as pl
from jax.experimental.pallas import tpu as pltpu
from jax.sharding import PartitionSpec as P

ITERS = 3
code_step = 0.1
epsilon = 1e-06

F32 = jnp.float32
BF16 = jnp.bfloat16
LANES = 128


def split3(x):
    high = x.astype(BF16).astype(F32)
    rest = x - high
    mid = rest.astype(BF16).astype(F32)
    return high, mid, rest - mid


def doubled(packed):
    n, half, width = packed.shape
    low = lax.broadcasted_iota(jnp.int32, packed.shape, 2) < width // 2
    swapped = jnp.concatenate([packed[..., width // 2:], packed[..., : width // 2]], axis=2)
    return jnp.concatenate([jnp.where(low, packed, swapped), jnp.where(low, swapped, packed)], axis=1).reshape(n * 2 * half, width)


def pack(twice):
    half, width = twice.shape[0] // 2, twice.shape[1]
    low = lax.broadcasted_iota(jnp.int32, (half, width), 1) < width // 2
    return jnp.where(low, twice[:half], twice[half:])


def factors(twice):
    low = lax.broadcasted_iota(jnp.int32, twice.shape, 1) < twice.shape[1] // 2
    norm = 0.5 * jnp.sum(twice * twice, axis=1, keepdims=True)
    return low, split3(twice), split3(norm)


def norm_lanes(norm, rows, first, second):
    lane = lax.broadcasted_iota(jnp.int32, (rows, LANES), 1)
    ones = jnp.where((lane >= second) & (lane < second + 3), 1.0, 0.0)
    n0, n1, n2 = norm
    return jnp.where(lane == first, n0, jnp.where(lane == first + 1, n1, jnp.where(lane == first + 2, n2, ones))).astype(BF16)


def row_side(twice):
    low, (h, m, l), norm = factors(twice)
    parts = [(-2.0 * h).astype(BF16), (-2.0 * m).astype(BF16), (-2.0 * jnp.where(low, h, l)).astype(BF16)]
    return jnp.concatenate(parts + [norm_lanes(norm, twice.shape[0], 3, 0)], axis=1)


def column_side(twice):
    low, (h, m, l), norm = factors(twice)
    hm = jnp.where(low, h, m).astype(BF16)
    gram = jnp.concatenate([hm, hm, jnp.where(low, l, h).astype(BF16), norm_lanes(norm, twice.shape[0], 0, 3)], axis=1)
    return gram, jnp.concatenate([hm, jnp.where(low, l, 1.0).astype(BF16)], axis=1)


def near_first(at, n):
    if n & (n - 1):
        return [lax.rem(at + k, n) for k in range(1, n)]
    flips = [(bit, bit * (1 - 2 * lax.rem(at // bit, 2))) for bit in (1 << i for i in range(n.bit_length() - 1))]
    return [at + sum(flip for bit, flip in flips if k & bit) for k in range(1, n)]


def far_first(at, n):
    low, high, found = 0, n - 1, []
    for _ in range(n - 1):
        pick = (2 * at - low - high + n) // n
        found.append(high + pick * (low - high))
        low, high = low + pick, high - 1 + pick
    return found


def kernel(n_blk, n_mem, coords, codes, classes, out,
           own, columns, band, weights, targets, code_tile, class_tile, gram_side, sum_side, part, part_in, wsum, wsum_in,
           load_sem, col_send, col_recv, band_send, band_recv, part_send, part_recv, w_send, w_recv):
    blk, mem = lax.axis_index("blk"), lax.axis_index("member")
    rows, width = coords.shape
    half = rows // 2
    slab = codes.shape[2]
    blks = near_first(blk, n_blk)
    mems = far_first(mem, n_mem)

    loads = [pltpu.make_async_copy(coords, out, load_sem.at[0]),
             pltpu.make_async_copy(classes.at[:, 0, :], class_tile, load_sem.at[1]),
             pltpu.make_async_copy(codes.at[:, 0, :], code_tile, load_sem.at[2])]
    for load in loads:
        load.start()
    barrier = pltpu.get_barrier_semaphore()
    for b in blks:
        pl.semaphore_signal(barrier, inc=1, device_id={"blk": b, "member": mem}, device_id_type=pl.DeviceIdType.MESH)
    for m in mems:
        pl.semaphore_signal(barrier, inc=1, device_id={"blk": blk, "member": m}, device_id_type=pl.DeviceIdType.MESH)

    def send(src, dst, ssem, rsem, b, m):
        return pltpu.make_async_remote_copy(src_ref=src, dst_ref=dst, send_sem=ssem, recv_sem=rsem,
                                            device_id={"blk": b, "member": m}, device_id_type=pl.DeviceIdType.MESH)

    def col_copy(it, b, slot):
        return send(own.at[it], columns.at[it, slot], col_send.at[it, b], col_recv.at[it, slot], b, mem)

    def band_copy(it, m, slot):
        return send(own.at[it], band.at[it, slot], band_send.at[it, m], band_recv.at[it, slot], blk, m)

    def part_copy(it, m, slot):
        return send(part.at[it, m], part_in.at[it, slot], part_send.at[it, m], part_recv.at[it, slot], blk, m)

    def w_copy(m, slot):
        return send(wsum.at[m], wsum_in.at[slot], w_send.at[m], w_recv.at[slot], blk, m)

    def spread(it, packed):
        own[it] = packed
        for m in mems:
            band_copy(it, m, mem).start()
        for b in reversed(blks):
            col_copy(it, b, blk).start()
        columns[it, blk] = packed
        band[it, mem] = packed

    loads[0].wait()
    start = out[...]
    first = jnp.concatenate([start[:half], start[half:]], axis=1)
    pl.semaphore_wait(barrier, n_blk + n_mem - 2)
    spread(0, first)

    loads[1].wait()
    loads[2].wait()
    order = mems + [mem]
    for m in order:
        at = pl.ds(pl.multiple_of(m * rows, rows), rows)
        row = lax.broadcasted_iota(jnp.int32, (rows, slab), 0)
        col = lax.broadcasted_iota(jnp.int32, (rows, slab), 1)
        self_at = jnp.where(m == mem, blk * rows, -slab - rows)
        weight = jnp.where(col == row + self_at, 0.0, 1.0 / (1.0 + class_tile[at, :].astype(F32)))
        weights[at, :] = weight
        targets[at, :] = weight * (code_tile[at, :].astype(F32) + 1.0) * code_step
        total = jnp.broadcast_to(jnp.sum(weight, axis=1, keepdims=True), (rows, 2 * width))
        wsum[m] = pack(total)
    for m in mems:
        w_copy(m, mem).start()

    for it in range(ITERS):
        arriving = [blk] + blks
        for pair in [arriving[:n_blk // 2], arriving[n_blk // 2:]]:
            for b in pair:
                if b is not blk:
                    col_copy(it, b, b).wait_recv()
            gram, sums = column_side(doubled(jnp.concatenate([columns[it, pl.ds(b, 1)] for b in pair], axis=0)))
            for k, b in enumerate(pair):
                block = pl.ds(pl.multiple_of(b * rows, rows), rows)
                gram_side[block, :], sum_side[block, :] = gram[k * rows:(k + 1) * rows], sums[k * rows:(k + 1) * rows]
        for m in mems:
            band_copy(it, m, m).wait_recv()
        for group in [mems, [mem]]:
            ats = [pl.ds(pl.multiple_of(m * rows, rows), rows) for m in group]
            twice = jnp.concatenate([doubled(band[it, pl.ds(m, 1)]) for m in group], axis=0)
            dist_sq = lax.dot_general(row_side(twice), gram_side[...], (((1,), (1,)), ((), ())), preferred_element_type=F32)
            target = jnp.concatenate([targets[at, :] for at in ats], axis=0)
            weight = jnp.concatenate([weights[at, :] for at in ats], axis=0)
            ratio = target * lax.rsqrt(jnp.maximum(dist_sq, 0.0) + epsilon)
            pull = weight - ratio
            high = pull.astype(BF16)
            low = (pull - high.astype(F32)).astype(BF16)
            sums = jnp.dot(jnp.concatenate([high, low], axis=0), sum_side[...], preferred_element_type=F32)
            sums = sums[:rows * len(group)] + sums[rows * len(group):]
            lane = lax.broadcasted_iota(jnp.int32, (rows * len(group), 2 * width), 1)
            extra = sums[:, 2 * width:]
            sums = sums[:, : 2 * width] + jnp.where(lane < width, extra, 0.0)
            sums = sums + jnp.concatenate([sums[:, width:], sums[:, :width]], axis=1)
            pulled = jnp.where(lane < width, jnp.concatenate([extra[:, width:], extra[:, :width]], axis=1), extra)
            for at, m in enumerate(group):
                span = slice(at * rows, (at + 1) * rows)
                packed = pack(sums[span]) + band[it, m] * (wsum[m] - pack(pulled[span]))
                if m is mem:
                    total = packed
                else:
                    part[it, m] = packed
                    part_copy(it, m, mem).start()
        if it == 0:
            weight_own = wsum[mem]
            for m in mems:
                w_copy(m, m).wait_recv()
                weight_own = weight_own + wsum_in[m]
            inverse = 1.0 / weight_own
        for m in mems:
            part_copy(it, m, m).wait_recv()
            total = total + part_in[it, m]
        total = total * inverse
        if it < ITERS - 1:
            spread(it + 1, total)
    out[...] = jnp.concatenate([total[:, :width], total[:, width:]], axis=0)

    for m in mems:
        w_copy(m, m).wait_send()
    for it in range(ITERS):
        for b in blks:
            col_copy(it, b, b).wait_send()
        for m in mems:
            band_copy(it, m, m).wait_send()
            part_copy(it, m, m).wait_send()


def body(n_blk, n_mem, coords, codes, classes):
    rows, width = coords.shape
    band_len, slab = rows * n_mem, rows * n_blk
    packed = (rows // 2, 2 * width)
    dma = pltpu.SemaphoreType.DMA
    return pl.pallas_call(
        functools.partial(kernel, n_blk, n_mem),
        out_shape=pltpu.VMEM((rows, width), F32),
        in_specs=[pl.BlockSpec(memory_space=pl.ANY)] * 3,
        out_specs=pl.BlockSpec(memory_space=pltpu.VMEM),
        scratch_shapes=[
            pltpu.VMEM((ITERS,) + packed, F32),
            pltpu.VMEM((ITERS, n_blk) + packed, F32),
            pltpu.VMEM((ITERS, n_mem) + packed, F32),
            pltpu.VMEM((band_len, slab), F32),
            pltpu.VMEM((band_len, slab), F32),
            pltpu.VMEM((band_len, slab), jnp.int32),
            pltpu.VMEM((band_len, slab), jnp.int32),
            pltpu.VMEM((slab, 4 * LANES), BF16),
            pltpu.VMEM((slab, 4 * width), BF16),
            pltpu.VMEM((ITERS, n_mem) + packed, F32),
            pltpu.VMEM((ITERS, n_mem) + packed, F32),
            pltpu.VMEM((n_mem,) + packed, F32),
            pltpu.VMEM((n_mem,) + packed, F32),
            dma((3,)),
            dma((ITERS, n_blk)), dma((ITERS, n_blk)),
            dma((ITERS, n_mem)), dma((ITERS, n_mem)),
            dma((ITERS, n_mem)), dma((ITERS, n_mem)),
            dma((n_mem,)), dma((n_mem,)),
        ],
        compiler_params=pltpu.CompilerParams(collective_id=0, has_side_effects=True),
        name="majorize",
    )(coords, codes, classes)


def solution(mesh):
    n_blk, n_mem = mesh.shape["blk"], mesh.shape["member"]
    in_specs = (P(("blk", "member"), None), P("blk", "member", None), P("blk", "member", None))
    out_specs = P(("blk", "member"), None)
    return jax.shard_map(functools.partial(body, n_blk, n_mem), mesh=mesh, in_specs=in_specs, out_specs=out_specs, check_vma=False)
```
